32 devices in a mesh: groups: 2 (over x), seq: 8 (over z, y), segment: 2 (over core).
Axes of the slice: x: 2, y: 2, z: 4, core: 2. Of those that a mesh axis runs over, the one named last changes fastest.
Arguments:
- queue_frames: bfloat16 [32, 32, 5120], P(('groups', 'segment'), 'seq'), parts along dimension 0, may hold values from -450 to 450
- fresh_frames: bfloat16 [2, 32, 5120], P('groups', 'seq'), parts along dimension 0, may hold values from -450 to 450
- slot_level: int32 [32], P(('groups', 'segment')), parts along dimension 0, may hold values from 0 to 49
- window_start: int32 [32], P(('groups', 'segment')), parts along dimension 0, may hold values from 0 to 3
- shift_table: float32 [50, 5120], replicated, may hold values from -3 to 3
- scale_table: float32 [50, 5120], replicated, may hold values from -1.5 to 1.5
- gate_table: float32 [50, 5120], replicated, may hold values from -10 to 10
- w_query: bfloat16 [5120, 4096], P(None, 'seq'), may hold values from -3.5 to 3.5
- w_key: bfloat16 [5120, 4096], P(None, 'seq'), may hold values from -3.5 to 3.5
- w_value: bfloat16 [5120, 4096], P(None, 'seq'), may hold values from -0.078125 to 0.078125
- w_out: bfloat16 [4096, 5120], P('seq'), may hold values from -0.5 to 0.5
- query_gain: float32 [4096], P('seq'), may hold values from 0.1 to 1.9
- key_gain: float32 [4096], P('seq'), may hold values from 0.1 to 1.9
Outputs:
- queue_out: bfloat16 [32, 32, 5120], P(('groups', 'segment'), 'seq'), parts along dimension 0
- departed: bfloat16 [4, 1, 32, 5120], P(('groups', 'segment'), None, 'seq'), parts along dimension 0
The draws below stay inside these ranges and needn't reach their ends.
There are 2 independent parts, one for each index of `groups`. The reference program is written for one: setup_inputs(seed, part) draws one part's arguments, and reference() takes and returns one part's arrays. A program takes and returns all parts, laid end to end along the dimension named above; an argument that names none is the same for every part. Nothing has to cross between parts.
All inputs are finite; a program needn't handle non-finite values.
Results may differ from the reference program's by a relative error of at most 0.02.
Values may be sent and summed in bfloat16 or wider, within the bound.
No kernel may reach another device: no remote copies, remote signals or barrier semaphores. Data moves between devices by JAX's collectives and lax.ppermute only.
A program may use at most 128 MiB of HBM per device.

```python
import math
import jax
import jax.numpy as jnp
from jax import lax

D = 5120
HD = 128
HEADS = 32
FRAMES = 8
KEYWIN = 4
LEVELS = 50
STEPS = 1
FTOK = 32
QUEUE = 16
INNER = 4096
N_SEQ = 8


def noise_field(key, frame_count):
    normal_key, channel_key, token_key = jax.random.split(key, 3)
    shape_all = (frame_count, FTOK, D)
    log_span = math.log(10.0)
    noise_rows = jnp.clip(jax.random.normal(normal_key, shape_all), -6.0, 6.0)
    ramp = jnp.arange(D, dtype=jnp.float32) / max(D - 1, 1)
    ramp_scale = jnp.exp(log_span * (ramp - 0.5))
    channel_scale = jnp.exp(jax.random.uniform(channel_key, (D,), minval=-0.7, maxval=0.7))
    token_scale = jnp.exp(jax.random.uniform(token_key, (frame_count, FTOK), minval=-0.5 * math.log(10.0), maxval=0.5 * math.log(10.0)))
    return noise_rows * (ramp_scale * channel_scale)[None, None, :] * token_scale[:, :, None]


def draw_queue_frames(key, part):
    noise_rows = noise_field(jax.random.fold_in(key, 11), QUEUE)
    return noise_rows.astype(jnp.bfloat16)


def draw_fresh_frames(key, part):
    return noise_field(jax.random.fold_in(key, 21), STEPS).astype(jnp.bfloat16)


def dense_weight(key, salt):
    inner_width = HEADS * HD
    base = jnp.clip(jax.random.normal(jax.random.fold_in(key, salt), (D, inner_width)), -6.0, 6.0)
    column_span = math.log(6.0)
    column_pos = jnp.arange(inner_width, dtype=jnp.float32) / max(inner_width - 1, 1)
    column_scale = jnp.exp(column_span * (column_pos - 0.5))
    return base * D ** (-0.5) * column_scale[None, :]


def draw_w_query(key, part):
    weight_rows = dense_weight(key, 31)
    return weight_rows.astype(jnp.bfloat16)


def draw_w_key(key, part):
    weight_rows = dense_weight(key, 41)
    return weight_rows.astype(jnp.bfloat16)


def touch_ends(values, own_key, smallest, top_value):
    spot = [jax.random.randint(jax.random.fold_in(own_key, axis), (), 0, length) for axis, length in enumerate(values.shape)]
    longest = values.shape.index(max(values.shape))
    next_to = spot[:longest] + [(spot[longest] + 1) % values.shape[longest]] + spot[longest + 1:]
    return values.at[tuple(spot)].set(smallest).at[tuple(next_to)].set(top_value)


def shard_levels(own_key, dims, cuts, smallest, top_value):
    loudness = 1.0
    for position, shards_of in cuts:
        steps = jax.random.uniform(jax.random.fold_in(jax.random.fold_in(own_key, 6), position), (shards_of,), jnp.float32, smallest / len(cuts), top_value / len(cuts))
        loudness = loudness * jnp.repeat(jnp.exp(steps), dims[position] // shards_of).reshape((-1,) + (1,) * (len(dims) - 1 - position))
    return loudness


def centred(rng, dims, scale, limit, shards=(), kind=jnp.bfloat16):
    drawn = scale * jax.random.normal(rng, dims, jnp.float32)
    if shards:
        drawn = drawn * shard_levels(rng, dims, shards, -0.22, 0.18)
    return jnp.clip(drawn, -limit, limit).astype(kind)


def setup_inputs(seed: int = 0, part: int = 0) -> dict:
    seeds = jax.random.split(jax.random.key(seed), 14)
    part_splits = jax.random.split(jax.random.fold_in(seeds[13], part), 14)
    queue_frames = draw_queue_frames(jax.random.fold_in(jax.random.fold_in(seeds[13], part), 71), part)
    fresh_frames = draw_fresh_frames(jax.random.fold_in(jax.random.fold_in(seeds[13], part), 71), part)
    slot_level = touch_ends(jax.random.randint(part_splits[2], (QUEUE,), 0, LEVELS), jax.random.fold_in(part_splits[2], 1), 0, LEVELS - 1).astype(jnp.int32)
    window_start = touch_ends(jax.random.randint(part_splits[3], (QUEUE,), 0, KEYWIN), jax.random.fold_in(part_splits[3], 1), 0, KEYWIN - 1).astype(jnp.int32)
    shift_table = centred(seeds[4], (LEVELS, D), 0.5, 3.0, (), jnp.float32)
    scale_table = centred(seeds[5], (LEVELS, D), 0.3, 1.5, (), jnp.float32)
    gate_table = centred(seeds[6], (LEVELS, D), 2.0, 10.0, (), jnp.float32)
    w_query = draw_w_query(jax.random.fold_in(seeds[13], 71), part)
    w_key = draw_w_key(jax.random.fold_in(seeds[13], 71), part)
    w_value = centred(seeds[9], (D, INNER), D ** -0.5, 0.078125, ((1, 8),))
    w_out = centred(seeds[10], (INNER, D), HD ** -0.5, 0.5, ((0, 8),))
    query_gain = jnp.clip(1.0 + 0.18 * jax.random.normal(seeds[11], (INNER,), jnp.float32), 0.1, 1.9)
    key_gain = jnp.clip(1.0 + 0.18 * jax.random.normal(seeds[12], (INNER,), jnp.float32), 0.1, 1.9)
    return dict(queue_frames=queue_frames, fresh_frames=fresh_frames, slot_level=slot_level, window_start=window_start, shift_table=shift_table, scale_table=scale_table, gate_table=gate_table, w_query=w_query, w_key=w_key, w_value=w_value, w_out=w_out, query_gain=query_gain, key_gain=key_gain)


epsilon = 1e-06
masked_score = -1e+30

def modulate(level_ids, lookup):
    onehot = (level_ids[:, None] == jnp.arange(lookup.shape[0], dtype=jnp.int32)[None, :]).astype(jnp.float32)
    return jnp.dot(onehot, lookup, precision=lax.Precision.HIGHEST)

def head_norm(raw, gain):
    inverse = lax.rsqrt(lax.optimization_barrier(jnp.mean(raw * raw, axis=1, keepdims=True)) + epsilon)
    return (raw * inverse * gain[None, :]).astype(jnp.bfloat16)

def attend_block(queries, key_rows, value_rows, usable):
    scores = jnp.einsum('qhd,khd->hqk', queries.astype(jnp.float32), key_rows.astype(jnp.float32)) * HD ** (-0.5)
    scores = jnp.where(usable[None, None, :], scores, masked_score)
    largest = lax.optimization_barrier(jnp.max(scores, axis=2, keepdims=True))
    lifted = jnp.exp(scores - largest)
    totals = lax.optimization_barrier(jnp.sum(lifted, axis=2, keepdims=True))
    weights = (lifted / totals).astype(jnp.bfloat16)
    return jnp.einsum('hqk,khd->qhd', weights.astype(jnp.float32), value_rows.astype(jnp.float32)).astype(jnp.bfloat16)

def layer_step(queue_state, slot_level, window_start, shift_table, scale_table, gate_table, w_query, w_key, w_value, w_out, query_gain, key_gain):
    queue_len = queue_state.shape[0]
    token_count = queue_state.shape[1]
    width = queue_state.shape[2]
    values_in = queue_state.astype(jnp.float32)
    inverse = lax.rsqrt(lax.optimization_barrier(jnp.mean(values_in * values_in, axis=2)) + epsilon)
    shift_rows = modulate(slot_level, shift_table)
    scale_rows = modulate(slot_level, scale_table)
    gate_rows = modulate(slot_level, gate_table)
    hidden = (values_in * inverse[:, :, None] * (1.0 + scale_rows[:, None]) + shift_rows[:, None]).astype(jnp.bfloat16)
    flat = hidden.reshape(queue_len * token_count, width)
    q_raw = jnp.dot(flat, w_query, preferred_element_type=jnp.float32)
    k_raw = jnp.dot(flat, w_key, preferred_element_type=jnp.float32)
    value_all = jnp.dot(flat, w_value, preferred_element_type=jnp.float32).astype(jnp.bfloat16)
    queries = head_norm(q_raw, query_gain).reshape(queue_len, token_count, HEADS, HD)
    key_all = head_norm(k_raw, key_gain).reshape(queue_len, token_count, HEADS, HD)
    value_all = value_all.reshape(queue_len, token_count, HEADS, HD)
    rim_width = KEYWIN - 1
    padding = ((rim_width, rim_width), (0, 0), (0, 0), (0, 0))
    key_pad = jnp.pad(key_all, padding)
    value_pad = jnp.pad(value_all, padding)

    def one_frame(frame_idx):
        window_begin = (frame_idx - window_start[frame_idx] + rim_width).astype(jnp.int32)
        key_rows = lax.dynamic_slice_in_dim(key_pad, window_begin, KEYWIN, 0).reshape(KEYWIN * token_count, HEADS, HD)
        value_rows = lax.dynamic_slice_in_dim(value_pad, window_begin, KEYWIN, 0).reshape(KEYWIN * token_count, HEADS, HD)
        frame_ids = window_begin - rim_width + jnp.arange(KEYWIN, dtype=jnp.int32)
        usable = jnp.repeat((frame_ids >= 0) & (frame_ids < queue_len), token_count)
        return attend_block(queries[frame_idx], key_rows, value_rows, usable)
    attended = lax.map(one_frame, jnp.arange(queue_len, dtype=jnp.int32))
    group_width = HEADS // N_SEQ * HD
    grouped = jnp.transpose(attended.reshape(queue_len * token_count, N_SEQ, group_width), (1, 0, 2))
    weight_groups = w_out.reshape(N_SEQ, group_width, width)

    def add_group(total, pair):
        rows, weight_rows = pair
        partial_value = jnp.dot(rows, weight_rows, preferred_element_type=jnp.float32).astype(jnp.bfloat16)
        partial_value = lax.optimization_barrier(partial_value)
        return (total + partial_value.astype(jnp.float32), None)
    start_total = jnp.zeros((queue_len * token_count, width), jnp.float32)
    projected, unused = lax.scan(add_group, start_total, (grouped, weight_groups))
    projected = projected.reshape(queue_len, token_count, width)
    return (values_in + gate_rows[:, None] * projected).astype(jnp.bfloat16)

def reference(queue_frames, fresh_frames, slot_level, window_start, shift_table, scale_table, gate_table, w_query, w_key, w_value, w_out, query_gain, key_gain):
    queue_state = queue_frames
    departed = []
    for step_idx in range(STEPS):
        updated = layer_step(queue_state, slot_level, window_start, shift_table, scale_table, gate_table, w_query, w_key, w_value, w_out, query_gain, key_gain)
        departed.append(updated[::FRAMES])
        queue_state = jnp.concatenate([updated[1:], fresh_frames[step_idx][None]], axis=0)
    return (queue_state, jnp.stack(departed, axis=1))
```

```python
import functools

import jax
import jax.numpy as jnp
from jax import lax
from jax.experimental import pallas as pl
from jax.experimental.pallas import tpu as pltpu
from jax.sharding import PartitionSpec as P

HD = 128
KEYWIN = 4


epsilon = 1e-06
masked_score = -1e30
VMEM_LIMIT = 16 << 20
WHOLE = pl.BlockSpec(memory_space=pltpu.VMEM)
SCALARS = pl.BlockSpec(memory_space=pltpu.SMEM)


def call(kernel, ins, outs, flops, scalars=0, scratch=(), limit=VMEM_LIMIT):
    moved = sum(x.size * x.dtype.itemsize for x in list(ins) + list(outs))
    return pl.pallas_call(
        kernel,
        in_specs=[SCALARS] * scalars + [WHOLE] * (len(ins) - scalars),
        out_specs=[WHOLE] * len(outs),
        out_shape=list(outs),
        scratch_shapes=list(scratch),
        compiler_params=pltpu.CompilerParams(vmem_limit_bytes=limit),
        cost_estimate=pl.CostEstimate(flops=flops, bytes_accessed=moved, transcendentals=0),
    )(*ins)


def like(shape, dtype=jnp.bfloat16):
    return jax.ShapeDtypeStruct(shape, dtype)


def rows_kernel(level_ref, *refs):
    tables, outs = refs[: len(refs) // 2], refs[len(refs) // 2 :]
    for f in range(outs[0].shape[0]):
        level = level_ref[f]
        for table, out in zip(tables, outs):
            out[f : f + 1, :] = table[pl.ds(level, 1), :]


def slot_rows(levels, tables):
    outs = [like((levels.shape[0], table.shape[1]), table.dtype) for table in tables]
    return call(rows_kernel, [levels, *tables], outs, 1000, scalars=1)


def place(column, first, total):
    rows = column.shape[0]
    lanes = lax.broadcasted_iota(jnp.int32, (rows, total), 1)
    picked = lanes == lax.broadcasted_iota(jnp.int32, (rows, total), 0) + first
    return jnp.sum(jnp.where(picked, column, 0.0), axis=0, keepdims=True)


def unplace(row, first, rows):
    total = row.shape[1]
    lanes = lax.broadcasted_iota(jnp.int32, (rows, total), 1)
    picked = lanes == lax.broadcasted_iota(jnp.int32, (rows, total), 0) + first
    return jnp.sum(jnp.where(picked, row, 0.0), axis=1, keepdims=True)


def row_of(position, offset, peers, rows):
    return pl.multiple_of(lax.rem(position + offset, peers) * rows, rows)


def project_kernel(first_frames, offsets, peers, position_ref, *refs):
    count = len(first_frames)
    x_refs, refs = refs[:count], refs[count:]
    scale_ref, shift_ref, wq_ref, wk_ref, wv_ref, gq_ref, gk_ref, q_ref, kv_ref, sq_ref, h_ref = refs
    row = 0
    for x_ref, first in zip(x_refs, first_frames):
        frames, tokens, width = x_ref.shape
        x = x_ref[...].astype(jnp.float32)
        inverse = lax.rsqrt(jnp.mean(x * x, axis=2, keepdims=True) + epsilon)
        scale = 1.0 + scale_ref[first : first + frames, :][:, None, :]
        shift = shift_ref[first : first + frames, :][:, None, :]
        hidden = (x * inverse * scale + shift).astype(jnp.bfloat16)
        h_ref[row : row + frames * tokens, :] = hidden.reshape(frames * tokens, width)
        row += frames * tokens
    rows = row // len(offsets)
    total = sq_ref.shape[1]
    hidden = h_ref[...]

    def squares_of(raw):
        column = jnp.sum(raw * raw, axis=1, keepdims=True)
        parts = [
            place(column[i * rows : (i + 1) * rows], row_of(position_ref[0], offset, peers, rows), total)
            for i, offset in enumerate(offsets)
        ]
        return sum(parts[1:], parts[0])

    q_raw = jnp.dot(hidden, wq_ref[...], preferred_element_type=jnp.float32)
    sq_ref[0:1, :] = squares_of(q_raw)
    q_ref[...] = (q_raw * gq_ref[...]).astype(jnp.bfloat16)
    k_raw = jnp.dot(hidden, wk_ref[...], preferred_element_type=jnp.float32)
    sq_ref[1:2, :] = squares_of(k_raw)
    kv_ref[0] = (k_raw * gk_ref[...]).astype(jnp.bfloat16)
    value = jnp.dot(hidden, wv_ref[...], preferred_element_type=jnp.float32)
    kv_ref[1] = value.astype(jnp.bfloat16)


def project(blocks, first_frames, offsets, peers, position, scale_rows, shift_rows, weights, gains):
    width, local = weights[0].shape
    rows = sum(x.shape[0] * x.shape[1] for x in blocks)
    total = rows // len(offsets) * peers
    return call(
        functools.partial(project_kernel, tuple(first_frames), tuple(offsets), peers),
        [position, *blocks, scale_rows, shift_rows, *weights, *gains],
        [like((rows, local)), like((2, rows, local)), like((2, total), jnp.float32)],
        6 * rows * width * local,
        scalars=1,
        scratch=[pltpu.VMEM((rows, width), jnp.bfloat16)],
    )


def gather_kernel(offsets, peers, rows, position_ref, *refs):
    kv_refs, out_ref = refs[:-1], refs[-1]
    for i, kv_ref in enumerate(kv_refs):
        base = i // len(offsets) * peers * rows
        for j, offset in enumerate(offsets[i % len(offsets)]):
            at = row_of(position_ref[0], offset, peers, rows)
            out_ref[:, pl.ds(base + at, rows), :] = kv_ref[:, j * rows : (j + 1) * rows, :]


def gather(sets, offsets, peers, rows, position):
    local = sets[0][0].shape[2]
    return call(
        functools.partial(gather_kernel, tuple(map(tuple, offsets)), peers, rows),
        [position, *(kv for kvs in sets for kv in kvs)],
        [like((2, len(sets) * peers * rows, local))],
        1000,
        scalars=1,
    )[0]


def attend_kernel(sizes, peers, inner, offsets, position_ref, start_ref, base_ref, q_ref, kv_ref, sq_ref, out_ref):
    frames, tokens, queue_len = sizes
    rows, local = q_ref.shape
    block = rows // len(offsets)
    columns = kv_ref.shape[1]
    total = sq_ref.shape[1]
    inverse_q_row = lax.rsqrt(sq_ref[0:1, :] / inner + epsilon)
    parts = [unplace(inverse_q_row, row_of(position_ref[0], offset, peers, block), block) for offset in offsets]
    inverse_q = parts[0] if len(parts) == 1 else jnp.concatenate(parts, axis=0)
    parts = [lax.rsqrt(sq_ref[1 + i : 2 + i, :] / inner + epsilon) for i in range(columns // total)]
    inverse_k = parts[0] if len(parts) == 1 else jnp.concatenate(parts, axis=1)
    row_frame = lax.broadcasted_iota(jnp.int32, (rows, columns), 0) // tokens % frames
    column = lax.broadcasted_iota(jnp.int32, (rows, columns), 1)
    column_frame = column // tokens % frames
    key_frame = column_frame + base_ref[0]
    for i in range(1, columns // total):
        key_frame = jnp.where(column >= i * total, column_frame + base_ref[i], key_frame)
    begin = row_frame + base_ref[0]
    for f in range(frames):
        begin = jnp.where(row_frame == f, begin - start_ref[f], begin)
    offset = key_frame - begin
    usable = (offset >= 0) & (offset < KEYWIN) & (key_frame >= 0) & (key_frame < queue_len)
    factor = inverse_q * inverse_k * HD ** (-0.5)
    for head in range(local // HD):
        lanes = slice(head * HD, (head + 1) * HD)
        scores = lax.dot_general(
            q_ref[:, lanes], kv_ref[0, :, lanes], (((1,), (1,)), ((), ())), preferred_element_type=jnp.float32
        )
        scores = jnp.where(usable, scores * factor, masked_score)
        lifted = jnp.exp(scores - jnp.max(scores, axis=1, keepdims=True))
        weights = (lifted / jnp.sum(lifted, axis=1, keepdims=True)).astype(jnp.bfloat16)
        out = jnp.dot(weights, kv_ref[1, :, lanes], preferred_element_type=jnp.float32)
        out_ref[:, lanes] = out.astype(jnp.bfloat16)


def attend(q, offsets, peers, position, kv, squares, window_start, bases, sizes, inner):
    rows, local = q.shape
    return call(
        functools.partial(attend_kernel, sizes, peers, inner, tuple(offsets)),
        [position, window_start, bases, q, kv, squares],
        [like((rows, local))],
        4 * rows * kv.shape[1] * local,
        scalars=3,
    )[0]


def partial_rows(att_ref, rows, w_ref):
    pieces = [att_ref[lo:hi, :] for lo, hi in rows]
    att = pieces[0] if len(pieces) == 1 else jnp.concatenate(pieces, axis=0)
    out = jnp.dot(att, w_ref[...], preferred_element_type=jnp.float32)
    return out.astype(jnp.bfloat16)


def first_sends_kernel(att_ref, w_ref, *outs):
    out = partial_rows(att_ref, [(0, att_ref.shape[0])], w_ref)
    size = outs[0].shape[0]
    for i, ref in enumerate(outs):
        ref[...] = out[i * size : (i + 1) * size]


def first_sends(att, w_out):
    quarter = like((att.shape[0] // 4, w_out.shape[1]))
    return call(first_sends_kernel, [att, w_out], [quarter] * 4, 2 * att.shape[0] * w_out.size)


def next_sends_kernel(half, rows, places, att_ref, w_ref, right_in, left_in, right_out, left_out):
    low = half * (rows // 2)
    spans = [(rows + low, rows + low + rows // 2), (low, low + rows // 2)]
    out = partial_rows(att_ref, spans, w_ref).astype(jnp.float32)
    for i, (arrived, ref) in enumerate(((right_in, right_out), (left_in, left_out))):
        own = out[i * (rows // 2) : (i + 1) * (rows // 2)]
        lo, hi = places[i]
        total = (own[lo:hi] + arrived[...].astype(jnp.float32)).astype(jnp.bfloat16)
        own = own.astype(jnp.bfloat16)
        parts = [x for x in (own[:lo], total, own[hi:]) if x.shape[0]]
        ref[...] = parts[0] if len(parts) == 1 else jnp.concatenate(parts, axis=0)


def next_sends(half, rows, places, att, w_out, right_in, left_in):
    out = like((rows // 2, w_out.shape[1]))
    return call(
        functools.partial(next_sends_kernel, half, rows, places),
        [att, w_out, right_in, left_in],
        [out, out],
        2 * rows * w_out.size,
    )


def finish_kernel(half, places, x_ref, gate_ref, att_ref, w_ref, right_in, left_in, out_ref):
    frames, tokens, width = out_ref.shape
    rows = frames * tokens
    own = partial_rows(att_ref, [(half * rows, half * rows + rows)], w_ref).astype(jnp.float32)
    for arrived, (lo, hi) in ((right_in, places[0]), (left_in, places[1])):
        added = own[lo:hi] + arrived[...].astype(jnp.float32)
        parts = [x for x in (own[:lo], added, own[hi:]) if x.shape[0]]
        own = parts[0] if len(parts) == 1 else jnp.concatenate(parts, axis=0)
    first = half * frames
    x = x_ref[first : first + frames].astype(jnp.float32)
    gate = gate_ref[first : first + frames, :][:, None, :]
    out_ref[...] = (x + gate * own.reshape(frames, tokens, width)).astype(jnp.bfloat16)


def finish(half, places, x, gate_rows, att, w_out, right_in, left_in):
    frames, tokens, width = x.shape
    return call(
        functools.partial(finish_kernel, half, places),
        [x, gate_rows, att, w_out, right_in, left_in],
        [like((frames // 2, tokens, width))],
        frames * tokens * w_out.size,
    )[0]


def shards(
    ring,
    queue_frames,
    fresh_frames,
    slot_level,
    window_start,
    shift_table,
    scale_table,
    gate_table,
    w_query,
    w_key,
    w_value,
    w_out,
    query_gain,
    key_gain,
):
    peers = lax.axis_size("seq")
    sections = lax.axis_size("segment")
    section = lax.axis_index("segment")
    frames, tokens, width = queue_frames.shape
    rows = frames * tokens
    half_frames = frames // 2
    queue_len = frames * sections
    local = w_query.shape[1]
    inner = local * peers
    far = peers // 2

    def right(x):
        return lax.ppermute(x, "seq", [(ring[i], ring[(i + 1) % peers]) for i in range(peers)])

    def left(x):
        return lax.ppermute(x, "seq", [(ring[(i + 1) % peers], ring[i]) for i in range(peers)])

    def from_sections(x):
        if sections == 2:
            return [lax.ppermute(x, "segment", [(0, 1), (1, 0)])]
        up = [(i, i + 1) for i in range(sections - 1)]
        return [lax.ppermute(x, "segment", route) for route in (up, [(j, i) for i, j in up])]

    if sections == 2:
        bases = jnp.stack([section, 1 - section])
    else:
        bases = jnp.stack([section, section - 1, section + 1])
    bases = bases.astype(jnp.int32) * frames

    place_in_ring = [ring.index(i) for i in range(peers)]
    position = jnp.asarray(place_in_ring, jnp.int32)[lax.axis_index("seq")][None]
    shift_rows, scale_rows, gate_rows = slot_rows(slot_level, [shift_table, scale_table, gate_table])
    weights = (w_query, w_key, w_value)
    gains = (query_gain[None], key_gain[None])

    def projected(blocks, first_frames, offsets):
        return project(blocks, first_frames, offsets, peers, position, scale_rows, shift_rows, weights, gains)

    from_left = from_right = queue_frames
    groups, offsets = [], [[0]]
    done = ([queue_frames], [0])
    for step in range(1, far + 1):
        if step < far:
            from_left, from_right = right(from_left), left(from_right)
            groups.append(projected(*done, offsets[-1]))
            done = ([from_left, from_right], [0, 0])
            offsets.append([peers - step, step])
        else:
            last = [right(from_left[:half_frames]), left(from_right[half_frames:])]
            groups.append(projected(*done, offsets[-1]))
            done = (last, [0, half_frames])
            offsets.append([far])
    groups.append(projected(*done, offsets[-1]))

    others = [from_sections(kv) for _, kv, _ in groups]
    squares = functools.reduce(jnp.add, [sq for _, _, sq in groups])
    squares = jnp.concatenate([squares] + from_sections(squares[1:2]), axis=0)
    distance = 1
    while distance < peers:
        pairs = [(i, i ^ distance) for i in range(peers)]
        squares = squares + lax.ppermute(squares, "seq", pairs)
        distance *= 2
    sets = [[kv for _, kv, _ in groups]] + [[other[i] for other in others] for i in range(len(others[0]))]
    kv = gather(sets, offsets, peers, rows, position)
    sizes = (frames, tokens, queue_len)

    def attended(i):
        return attend(groups[i][0], offsets[i], peers, position, kv, squares, window_start, bases, sizes, inner)

    quarter = rows // 4
    sends = first_sends(attended(far), w_out)
    carried = [(right(sends[0]), left(sends[1])), (right(sends[2]), left(sends[3]))]
    places = ((0, quarter), (quarter, 2 * quarter))
    for step in range(far - 1, 0, -1):
        att = attended(step)
        for half in range(2):
            out = next_sends(half, rows, places, att, w_out, *carried[half])
            carried[half] = (right(out[0]), left(out[1]))
        places = ((0, 2 * quarter), (0, 2 * quarter))
    att = attended(0)
    near = finish(0, places, queue_frames, gate_rows, att, w_out, *carried[0])
    handed = lax.ppermute(near[0], "segment", [(i, i - 1) for i in range(1, sections)])
    later = finish(1, places, queue_frames, gate_rows, att, w_out, *carried[1])
    arriving = jnp.where(section == sections - 1, fresh_frames[0], handed)
    queue_state = jnp.concatenate([near[1:], later, arriving[None]], axis=0)
    return (queue_state, near[0][None, None])


def ring_order(mesh):
    axes = list(mesh.axis_names)
    index = [0] * len(axes)
    index[axes.index("seq")] = slice(None)
    places = [tuple(d.coords) for d in mesh.devices[tuple(index)]]
    spread = [d for d in range(3) if len({p[d] for p in places}) > 1]
    at = {tuple(p[d] for d in spread): i for i, p in enumerate(places)}
    if len(spread) == 1:
        return [at[key] for key in sorted(at)]
    if len(spread) == 2:
        spans = [sorted({key[i] for key in at}) for i in range(2)]
        long = 0 if len(spans[0]) % 2 == 0 else 1
        if len(spans[long]) % 2 == 0 and len(at) == len(spans[0]) * len(spans[1]):
            outward, across = spans[long], spans[1 - long]
            path = []
            for i, a in enumerate(outward):
                turn = across[1:] if i % 2 == 0 else across[:0:-1]
                path += [(a, b) for b in turn]
            path += [(a, across[0]) for a in reversed(outward)]
            return [at[key if long == 0 else key[::-1]] for key in path]
    return list(range(len(places)))


def solution(mesh):
    return jax.shard_map(
        functools.partial(shards, ring_order(mesh)),
        mesh=mesh,
        in_specs=(
            P(("groups", "segment"), "seq", None),
            P("groups", "seq", None),
            P(("groups", "segment")),
            P(("groups", "segment")),
            P(),
            P(),
            P(),
            P(None, "seq"),
            P(None, "seq"),
            P(None, "seq"),
            P("seq", None),
            P("seq"),
            P("seq"),
        ),
        out_specs=(
            P(("groups", "segment"), "seq", None),
            P(("groups", "segment"), None, "seq", None),
        ),
        check_vma=False,
    )
```

```python
import functools

import jax
import jax.numpy as jnp
from jax import lax
from jax.experimental import pallas as pl
from jax.experimental.pallas import tpu as pltpu
from jax.sharding import PartitionSpec as P

HD = 128
KEYWIN = 4


epsilon = 1e-06
masked_score = -1e30
VMEM_LIMIT = 16 << 20
WHOLE = pl.BlockSpec(memory_space=pltpu.VMEM)
SCALARS = pl.BlockSpec(memory_space=pltpu.SMEM)


def call(kernel, ins, outs, flops, scalars=0, scratch=(), limit=VMEM_LIMIT):
    moved = sum(x.size * x.dtype.itemsize for x in list(ins) + list(outs))
    return pl.pallas_call(
        kernel,
        in_specs=[SCALARS] * scalars + [WHOLE] * (len(ins) - scalars),
        out_specs=[WHOLE] * len(outs),
        out_shape=list(outs),
        scratch_shapes=list(scratch),
        compiler_params=pltpu.CompilerParams(vmem_limit_bytes=limit),
        cost_estimate=pl.CostEstimate(flops=flops, bytes_accessed=moved, transcendentals=0),
    )(*ins)


def like(shape, dtype=jnp.bfloat16):
    return jax.ShapeDtypeStruct(shape, dtype)


def after(arrived, done):
    return lax.optimization_barrier((arrived, done))


def prepare_kernel(tables, count, level_ref, *refs):
    ins, refs = refs[: tables + count], refs[tables + count :]
    rows, kept, scratch, sems = refs[:tables], refs[tables : tables + count], refs[tables + count : -1], refs[-1]
    copies = [
        pltpu.make_async_copy(src, dst, sems.at[i]) for i, (src, dst) in enumerate(zip(ins, (*scratch, *kept)))
    ]
    for copy in copies:
        copy.start()
    for copy in copies[:tables]:
        copy.wait()
    for f in range(rows[0].shape[0]):
        level = level_ref[f]
        for table, out in zip(scratch, rows):
            out[f : f + 1, :] = table[pl.ds(level, 1), :]
    for copy in copies[tables:]:
        copy.wait()


def prepare(levels, tables, arrays):
    anywhere = pl.BlockSpec(memory_space=pl.ANY)
    outs = [like((levels.shape[0], table.shape[1]), table.dtype) for table in tables]
    outs += [like(x.shape, x.dtype) for x in arrays]
    moved = sum(x.size * x.dtype.itemsize for x in (*tables, *arrays))
    return pl.pallas_call(
        functools.partial(prepare_kernel, len(tables), len(arrays)),
        in_specs=[SCALARS] + [anywhere] * (len(tables) + len(arrays)),
        out_specs=[WHOLE] * len(outs),
        out_shape=outs,
        scratch_shapes=[pltpu.VMEM(x.shape, x.dtype) for x in tables]
        + [pltpu.SemaphoreType.DMA((len(tables) + len(arrays),))],
        compiler_params=pltpu.CompilerParams(vmem_limit_bytes=32 << 20),
        cost_estimate=pl.CostEstimate(flops=1000, bytes_accessed=moved, transcendentals=0),
    )(levels, *tables, *arrays)


def place(column, first, total):
    rows = column.shape[0]
    lanes = lax.broadcasted_iota(jnp.int32, (rows, total), 1)
    picked = lanes == lax.broadcasted_iota(jnp.int32, (rows, total), 0) + first
    return jnp.sum(jnp.where(picked, column, 0.0), axis=0, keepdims=True)


def unplace(row, first, rows):
    total = row.shape[1]
    lanes = lax.broadcasted_iota(jnp.int32, (rows, total), 1)
    picked = lanes == lax.broadcasted_iota(jnp.int32, (rows, total), 0) + first
    return jnp.sum(jnp.where(picked, row, 0.0), axis=1, keepdims=True)


def row_of(ring, offset, rows):
    index = lax.axis_index("seq")
    first = jnp.int32(0)
    for i, device in enumerate(ring):
        first = jnp.where(index == device, (i + offset) % len(ring) * rows, first)
    return pl.multiple_of(first, rows)


def project_kernel(first_frames, offsets, ring, *refs):
    count = len(first_frames)
    x_refs, refs = refs[:count], refs[count:]
    scale_ref, shift_ref, wq_ref, wk_ref, wv_ref, gq_ref, gk_ref, q_ref, kv_ref, sq_ref, h_ref = refs
    row = 0
    for x_ref, first in zip(x_refs, first_frames):
        frames, tokens, width = x_ref.shape
        x = x_ref[...].astype(jnp.float32)
        inverse = lax.rsqrt(jnp.mean(x * x, axis=2, keepdims=True) + epsilon)
        scale = 1.0 + scale_ref[first : first + frames, :][:, None, :]
        shift = shift_ref[first : first + frames, :][:, None, :]
        hidden = (x * inverse * scale + shift).astype(jnp.bfloat16)
        h_ref[row : row + frames * tokens, :] = hidden.reshape(frames * tokens, width)
        row += frames * tokens
    rows = row // len(offsets)
    total = sq_ref.shape[1]
    hidden = h_ref[...]

    def squares_of(raw):
        column = jnp.sum(raw * raw, axis=1, keepdims=True)
        parts = [
            place(column[i * rows : (i + 1) * rows], row_of(ring, offset, rows), total)
            for i, offset in enumerate(offsets)
        ]
        return sum(parts[1:], parts[0])

    q_raw = jnp.dot(hidden, wq_ref[...], preferred_element_type=jnp.float32)
    sq_ref[0:1, :] = squares_of(q_raw)
    q_ref[...] = (q_raw * gq_ref[...]).astype(jnp.bfloat16)
    k_raw = jnp.dot(hidden, wk_ref[...], preferred_element_type=jnp.float32)
    sq_ref[1:2, :] = squares_of(k_raw)
    kv_ref[0] = (k_raw * gk_ref[...]).astype(jnp.bfloat16)
    value = jnp.dot(hidden, wv_ref[...], preferred_element_type=jnp.float32)
    kv_ref[1] = value.astype(jnp.bfloat16)


def project(blocks, offsets, first_frames, ring, scale_rows, shift_rows, weights):
    width, local = weights[0].shape
    offsets = dict.fromkeys(offsets)
    rows = sum(x.shape[0] * x.shape[1] for x in blocks)
    total = rows // len(offsets) * len(ring)
    return call(
        functools.partial(project_kernel, tuple(first_frames), tuple(offsets), ring),
        [*blocks, scale_rows, shift_rows, *weights],
        [like((rows, local)), like((2, rows, local)), like((2, total), jnp.float32)],
        6 * rows * width * local,
        scratch=[pltpu.VMEM((rows, width), jnp.bfloat16)],
    )


def gather_kernel(offsets, ring, rows, *refs):
    kv_refs, out_ref = refs[:-1], refs[-1]
    for i, kv_ref in enumerate(kv_refs):
        base = i // len(offsets) * len(ring) * rows
        for j, offset in enumerate(offsets[i % len(offsets)]):
            at = row_of(ring, offset, rows)
            out_ref[:, pl.ds(base + at, rows), :] = kv_ref[:, j * rows : (j + 1) * rows, :]


def gather(sets, offsets, ring, rows):
    local = sets[0][0].shape[2]
    return call(
        functools.partial(gather_kernel, tuple(map(tuple, offsets)), ring, rows),
        [kv for kvs in sets for kv in kvs],
        [like((2, len(sets) * len(ring) * rows, local))],
        1000,
    )[0]


def attend_kernel(sizes, ring, inner, offsets, start_ref, *refs):
    frames, tokens, sections = sizes
    q_refs, (kv_ref, sq_ref, out_ref) = refs[:-3], refs[-3:]
    rows, local = out_ref.shape
    block = rows // len(offsets)
    columns = kv_ref.shape[1]
    total = sq_ref.shape[1]
    inverse_q_row = lax.rsqrt(sq_ref[0:1, :] / inner + epsilon)
    parts = [unplace(inverse_q_row, row_of(ring, offset, block), block) for offset in offsets]
    inverse_q = parts[0] if len(parts) == 1 else jnp.concatenate(parts, axis=0)
    parts = [lax.rsqrt(sq_ref[1 + i : 2 + i, :] / inner + epsilon) for i in range(columns // total)]
    inverse_k = parts[0] if len(parts) == 1 else jnp.concatenate(parts, axis=1)
    section = lax.axis_index("segment")
    if sections == 2:
        bases = [section, 1 - section]
    else:
        bases = [section, section - 1, section + 1]
    row_frame = lax.broadcasted_iota(jnp.int32, (rows, 1), 0) // tokens % frames
    column = lax.broadcasted_iota(jnp.int32, (1, columns), 1)
    column_frame = column // tokens % frames
    key_frame = column_frame + bases[0] * frames
    for i in range(1, columns // total):
        key_frame = jnp.where(column >= i * total, column_frame + bases[i] * frames, key_frame)
    begin = row_frame + section * frames
    for f in range(frames):
        begin = jnp.where(row_frame == f, begin - start_ref[f], begin)
    key_frame = jnp.where((key_frame >= 0) & (key_frame < frames * sections), key_frame, -frames)
    usable = (key_frame >= begin) & (key_frame < begin + KEYWIN)
    usable &= jnp.broadcast_to(key_frame >= 0, usable.shape)
    inverse_q = inverse_q * HD ** (-0.5)
    for head in range(local // HD):
        lanes = slice(head * HD, (head + 1) * HD)
        parts = [q_ref[:, lanes] for q_ref in q_refs]
        q = parts[0] if len(parts) == 1 else jnp.concatenate(parts, axis=0)
        scores = lax.dot_general(
            q, kv_ref[0, :, lanes], (((1,), (1,)), ((), ())), preferred_element_type=jnp.float32
        )
        scores = jnp.where(usable, scores * inverse_q * inverse_k, masked_score)
        lifted = jnp.exp(scores - jnp.max(scores, axis=1, keepdims=True))
        weights = (lifted * (1.0 / jnp.sum(lifted, axis=1, keepdims=True))).astype(jnp.bfloat16)
        out = jnp.dot(weights, kv_ref[1, :, lanes], preferred_element_type=jnp.float32)
        out_ref[:, lanes] = out.astype(jnp.bfloat16)


def attend(queries, offsets, ring, kv, squares, window_start, sizes, inner):
    rows, local = sum(q.shape[0] for q in queries), queries[0].shape[1]
    return call(
        functools.partial(attend_kernel, sizes, ring, inner, tuple(offsets)),
        [window_start, *queries, kv, squares],
        [like((rows, local))],
        4 * rows * kv.shape[1] * local,
        scalars=1,
    )[0]


def partial_kernel(row, att_ref, w_ref, *outs):
    rows = sum(ref.shape[0] for ref in outs)
    out = jnp.dot(att_ref[row : row + rows, :], w_ref[...], preferred_element_type=jnp.float32)
    row = 0
    for ref in outs:
        ref[...] = out[row : row + ref.shape[0]].astype(jnp.bfloat16)
        row += ref.shape[0]


def partials(att, row, w_out, sizes):
    return call(
        functools.partial(partial_kernel, row),
        [att, w_out],
        [like((size, w_out.shape[1])) for size in sizes],
        2 * sum(sizes) * w_out.size,
    )


def added(own, arrived, lo):
    hi = lo + arrived.shape[0]
    total = own[lo:hi] + arrived.astype(jnp.float32)
    parts = [x for x in (own[:lo], total, own[hi:]) if x.shape[0]]
    return parts[0] if len(parts) == 1 else jnp.concatenate(parts, axis=0)


def next_sends_kernel(rows, places, right_own, left_own, right_in, left_in, right_out, left_out):
    low, high = rows
    pairs = ((right_own, right_in, right_out), (left_own, left_in, left_out))
    for at, (own, arrived, out) in zip(places, pairs):
        total = added(own[low:high, :].astype(jnp.float32), arrived[...], at)
        out[...] = total.astype(jnp.bfloat16)


def next_sends(half, places, right_own, left_own, right_in, left_in):
    rows = right_own.shape[0] // 2
    out = like((rows, right_own.shape[1]))
    return call(
        functools.partial(next_sends_kernel, (half * rows, half * rows + rows), places),
        [right_own, left_own, right_in, left_in],
        [out, out],
        4 * rows * right_own.shape[1],
    )


def updated_half(half, places, x_ref, gate_ref, own_ref, right_in, left_in):
    frames, tokens, width = x_ref.shape
    frames = frames // 2
    rows = frames * tokens
    own = own_ref[half * rows : half * rows + rows, :].astype(jnp.float32)
    own = added(added(own, right_in[...], places[0]), left_in[...], places[1])
    first = half * frames
    x = x_ref[first : first + frames].astype(jnp.float32)
    gate = gate_ref[first : first + frames, :][:, None, :]
    return (x + gate * own.reshape(frames, tokens, width)).astype(jnp.bfloat16)


def near_kernel(places, x_ref, gate_ref, own_ref, right_in, left_in, first_ref, rest_ref):
    out = updated_half(0, places, x_ref, gate_ref, own_ref, right_in, left_in)
    first_ref[...] = out[0]
    rest_ref[...] = out[1:]


def near_half(places, x, gate_rows, own, right_in, left_in):
    frames, tokens, width = x.shape
    return call(
        functools.partial(near_kernel, places),
        [x, gate_rows, own, right_in, left_in],
        [like((tokens, width)), like((frames // 2 - 1, tokens, width))],
        4 * x.size,
    )


def last_kernel(places, sections, x_ref, gate_ref, own_ref, right_in, left_in, rest_ref, handed_ref, fresh_ref, out_ref):
    frames = out_ref.shape[0]
    out = updated_half(1, places, x_ref, gate_ref, own_ref, right_in, left_in)
    out_ref[: frames // 2 - 1] = rest_ref[...]
    out_ref[frames // 2 - 1 : frames - 1] = out
    newest = lax.axis_index("segment") == sections - 1

    @pl.when(newest)
    def _():
        out_ref[frames - 1 :] = fresh_ref[...]

    @pl.when(jnp.logical_not(newest))
    def _():
        out_ref[frames - 1] = handed_ref[...]


def last_half(places, sections, x, gate_rows, own, right_in, left_in, rest, handed, fresh):
    return call(
        functools.partial(last_kernel, places, sections),
        [x, gate_rows, own, right_in, left_in, rest, handed, fresh],
        [like(x.shape)],
        4 * x.size,
    )[0]


def shards(
    ring,
    queue_frames,
    fresh_frames,
    slot_level,
    window_start,
    shift_table,
    scale_table,
    gate_table,
    w_query,
    w_key,
    w_value,
    w_out,
    query_gain,
    key_gain,
):
    peers = lax.axis_size("seq")
    sections = lax.axis_size("segment")
    frames, tokens, width = queue_frames.shape
    rows = frames * tokens
    half_frames = frames // 2
    local = w_query.shape[1]
    inner = local * peers
    far = peers // 2

    def right(x):
        return lax.ppermute(x, "seq", [(ring[i], ring[(i + 1) % peers]) for i in range(peers)])

    def left(x):
        return lax.ppermute(x, "seq", [(ring[(i + 1) % peers], ring[i]) for i in range(peers)])

    def from_sections(x):
        if sections == 2:
            return [lax.ppermute(x, "segment", [(0, 1), (1, 0)])]
        up = [(i, i + 1) for i in range(sections - 1)]
        return [lax.ppermute(x, "segment", route) for route in (up, [(j, i) for i, j in up])]

    from_left = from_right = queue_frames
    groups, offsets, waiting = [], [], [(queue_frames, 0, 0)]
    for step in range(1, far + 1):
        if step < far:
            arrived = right(from_left), left(from_right)
            news = [(peers - step, 0), (step, 0)]
        else:
            arrived = right(from_left[:half_frames]), left(from_right[half_frames:])
            news = [(far, 0), (far, half_frames)]
        if step == 1:
            prepared = prepare(
                slot_level,
                [shift_table, scale_table, gate_table],
                [w_query, w_key, w_value, query_gain[None], key_gain[None]],
            )
            arrived, prepared = after(arrived, prepared)
            shift_rows, scale_rows, gate_rows, *weights = prepared
        else:
            groups.append(project(*zip(*waiting), ring, scale_rows, shift_rows, weights))
            offsets.append(list(dict.fromkeys(offset for _, offset, _ in waiting)))
            waiting = []
            arrived, groups[-1] = after(arrived, groups[-1])
        from_left, from_right = arrived
        waiting += [(x, *new) for x, new in zip(arrived, news)]
    groups.append(project(*zip(*waiting), ring, scale_rows, shift_rows, weights))
    offsets.append(list(dict.fromkeys(offset for _, offset, _ in waiting)))

    others = [from_sections(kv) for _, kv, _ in groups]
    squares = functools.reduce(jnp.add, [sq for _, _, sq in groups])
    squares = jnp.concatenate([squares] + from_sections(squares[1:2]), axis=0)
    distance = 1
    while distance < peers:
        pairs = [(i, i ^ distance) for i in range(peers)]
        squares = squares + lax.ppermute(squares, "seq", pairs)
        distance *= 2
    sets = [[kv for _, kv, _ in groups]] + [[other[i] for other in others] for i in range(len(others[0]))]
    kv = gather(sets, offsets, ring, rows)
    sizes = (frames, tokens, sections)

    att = attend([q for q, _, _ in groups], sum(offsets, []), ring, kv, squares, window_start, sizes, inner)

    quarter = rows // 4
    order = [offset for offset in sum(offsets, [])]
    sends = partials(att, order.index(far) * rows, w_out, [quarter] * 4)
    carried = [(right(sends[0]), left(sends[1])), (right(sends[2]), left(sends[3]))]
    own = dict(zip(order, partials(att, 0, w_out, [rows] * (peers - 1))))
    places = (0, quarter)
    for step in range(far - 1, 0, -1):
        for half in range(2):
            out = next_sends(half, places, own[step], own[peers - step], *carried[half])
            carried[half] = (right(out[0]), left(out[1]))
        places = (0, 0)
    first, rest = near_half(places, queue_frames, gate_rows, own[0], *carried[0])
    handed = lax.ppermute(first, "segment", [(i, i - 1) for i in range(1, sections)])
    queue_state = last_half(
        places, sections, queue_frames, gate_rows, own[0], *carried[1], rest, handed, fresh_frames
    )
    return (queue_state, first[None, None])


def ring_order(mesh):
    axes = list(mesh.axis_names)
    index = [0] * len(axes)
    index[axes.index("seq")] = slice(None)
    places = [tuple(d.coords) for d in mesh.devices[tuple(index)]]
    spread = [d for d in range(3) if len({p[d] for p in places}) > 1]
    at = {tuple(p[d] for d in spread): i for i, p in enumerate(places)}
    if len(spread) == 1:
        return [at[key] for key in sorted(at)]
    if len(spread) == 2:
        spans = [sorted({key[i] for key in at}) for i in range(2)]
        long = 0 if len(spans[0]) % 2 == 0 else 1
        if len(spans[long]) % 2 == 0 and len(at) == len(spans[0]) * len(spans[1]):
            outward, across = spans[long], spans[1 - long]
            path = []
            for i, a in enumerate(outward):
                turn = across[1:] if i % 2 == 0 else across[:0:-1]
                path += [(a, b) for b in turn]
            path += [(a, across[0]) for a in reversed(outward)]
            return [at[key if long == 0 else key[::-1]] for key in path]
    return list(range(len(places)))


def solution(mesh):
    return jax.shard_map(
        functools.partial(shards, tuple(ring_order(mesh))),
        mesh=mesh,
        in_specs=(
            P(("groups", "segment"), "seq", None),
            P("groups", "seq", None),
            P(("groups", "segment")),
            P(("groups", "segment")),
            P(),
            P(),
            P(),
            P(None, "seq"),
            P(None, "seq"),
            P(None, "seq"),
            P("seq", None),
            P("seq"),
            P("seq"),
        ),
        out_specs=(
            P(("groups", "segment"), "seq", None),
            P(("groups", "segment"), None, "seq", None),
        ),
        check_vma=False,
    )
```

```python
import functools

import jax
import jax.numpy as jnp
from jax import lax
from jax.experimental import pallas as pl
from jax.experimental.pallas import tpu as pltpu
from jax.sharding import PartitionSpec as P

HD = 128
KEYWIN = 4


epsilon = 1e-06
masked_score = -1e30
VMEM_LIMIT = 16 << 20
WHOLE = pl.BlockSpec(memory_space=pltpu.VMEM)
SCALARS = pl.BlockSpec(memory_space=pltpu.SMEM)


def call(kernel, ins, outs, flops, scalars=0, scratch=(), limit=VMEM_LIMIT):
    moved = sum(x.size * x.dtype.itemsize for x in list(ins) + list(outs))
    return pl.pallas_call(
        kernel,
        in_specs=[SCALARS] * scalars + [WHOLE] * (len(ins) - scalars),
        out_specs=[WHOLE] * len(outs),
        out_shape=list(outs),
        scratch_shapes=list(scratch),
        compiler_params=pltpu.CompilerParams(vmem_limit_bytes=limit),
        cost_estimate=pl.CostEstimate(flops=flops, bytes_accessed=moved, transcendentals=0),
    )(*ins)


def like(shape, dtype=jnp.bfloat16):
    return jax.ShapeDtypeStruct(shape, dtype)


def after(arrived, done):
    return lax.optimization_barrier((arrived, done))


def prepare_kernel(tables, count, level_in, *refs):
    ins, refs = refs[: tables + count], refs[tables + count :]
    rows, kept, scratch = refs[:tables], refs[tables : tables + count], refs[tables + count : 2 * tables + count]
    level_ref, sems = refs[2 * tables + count :]
    pairs = [(level_in, level_ref), *zip(ins, (*scratch, *kept))]
    copies = [pltpu.make_async_copy(src, dst, sems.at[i]) for i, (src, dst) in enumerate(pairs)]
    for copy in copies:
        copy.start()
    for copy in copies[: tables + 1]:
        copy.wait()
    for f in range(rows[0].shape[0]):
        level = level_ref[f]
        for table, out in zip(scratch, rows):
            out[f : f + 1, :] = table[pl.ds(level, 1), :]
    for copy in copies[tables + 1 :]:
        copy.wait()


def prepare(levels, tables, arrays, limit=VMEM_LIMIT):
    in_hbm = pl.BlockSpec(memory_space=pltpu.HBM)
    outs = [like((levels.shape[0], table.shape[1]), table.dtype) for table in tables]
    outs += [like(x.shape, x.dtype) for x in arrays]
    moved = sum(x.size * x.dtype.itemsize for x in (*tables, *arrays))
    return pl.pallas_call(
        functools.partial(prepare_kernel, len(tables), len(arrays)),
        in_specs=[in_hbm] * (1 + len(tables) + len(arrays)),
        out_specs=[WHOLE] * len(outs),
        out_shape=outs,
        scratch_shapes=[pltpu.VMEM(x.shape, x.dtype) for x in tables]
        + [pltpu.SMEM(levels.shape, levels.dtype), pltpu.SemaphoreType.DMA((1 + len(tables) + len(arrays),))],
        compiler_params=pltpu.CompilerParams(vmem_limit_bytes=limit),
        cost_estimate=pl.CostEstimate(flops=1000, bytes_accessed=moved, transcendentals=0),
    )(*(pltpu.with_memory_space_constraint(x, pltpu.HBM) for x in (levels, *tables, *arrays)))


def place(column, first, total):
    rows = column.shape[0]
    lanes = lax.broadcasted_iota(jnp.int32, (rows, total), 1)
    picked = lanes == lax.broadcasted_iota(jnp.int32, (rows, total), 0) + first
    return jnp.sum(jnp.where(picked, column, 0.0), axis=0, keepdims=True)


def unplace(row, first, rows):
    total = row.shape[1]
    lanes = lax.broadcasted_iota(jnp.int32, (rows, total), 1)
    picked = lanes == lax.broadcasted_iota(jnp.int32, (rows, total), 0) + first
    return jnp.sum(jnp.where(picked, row, 0.0), axis=1, keepdims=True)


def row_of(ring, offset, rows):
    index = lax.axis_index("seq")
    first = jnp.int32(0)
    for i, device in enumerate(ring):
        first = jnp.where(index == device, (i + offset) % len(ring) * rows, first)
    return pl.multiple_of(first, rows)


def project_kernel(first_frames, offsets, ring, *refs):
    count = len(first_frames)
    x_refs, refs = refs[:count], refs[count:]
    scale_ref, shift_ref, wq_ref, wk_ref, q_ref, k_ref, sq_ref, h_ref = refs
    row = 0
    for x_ref, first in zip(x_refs, first_frames):
        frames, tokens, width = x_ref.shape
        x = x_ref[...].astype(jnp.float32)
        inverse = lax.rsqrt(jnp.mean(x * x, axis=2, keepdims=True) + epsilon)
        scale = 1.0 + scale_ref[first : first + frames, :][:, None, :]
        shift = shift_ref[first : first + frames, :][:, None, :]
        hidden = (x * inverse * scale + shift).astype(jnp.bfloat16)
        h_ref[row : row + frames * tokens, :] = hidden.reshape(frames * tokens, width)
        row += frames * tokens
    rows = row // len(offsets)
    total = sq_ref.shape[1]
    hidden = h_ref[...]

    def squares_of(raw):
        column = jnp.sum(raw * raw, axis=1, keepdims=True)
        parts = [
            place(column[i * rows : (i + 1) * rows], row_of(ring, offset, rows), total)
            for i, offset in enumerate(offsets)
        ]
        return sum(parts[1:], parts[0])

    q_raw = jnp.dot(hidden, wq_ref[...], preferred_element_type=jnp.float32)
    sq_ref[0:1, :] = squares_of(q_raw)
    q_ref[...] = q_raw
    k_raw = jnp.dot(hidden, wk_ref[...], preferred_element_type=jnp.float32)
    sq_ref[1:2, :] = squares_of(k_raw)
    k_ref[...] = k_raw


def project(blocks, offsets, first_frames, ring, scale_rows, shift_rows, weights):
    w_query, w_key = weights
    width, local = w_query.shape
    offsets = dict.fromkeys(offsets)
    rows = sum(x.shape[0] * x.shape[1] for x in blocks)
    total = rows // len(offsets) * len(ring)
    return call(
        functools.partial(project_kernel, tuple(first_frames), tuple(offsets), ring),
        [*blocks, scale_rows, shift_rows, w_query, w_key],
        [like((rows, local), jnp.float32)] * 2 + [like((2, total), jnp.float32), like((rows, width))],
        4 * rows * width * local,
    )


def finish_projection_kernel(count, *refs):
    q_refs, k_refs, h_refs = (refs[i * count : (i + 1) * count] for i in range(3))
    wv_ref, gq_ref, gk_ref, q_out, kv_out = refs[3 * count :]
    row = 0
    for q_ref, k_ref in zip(q_refs, k_refs):
        end = row + q_ref.shape[0]
        q_out[row:end, :] = (q_ref[...] * gq_ref[...]).astype(jnp.bfloat16)
        kv_out[0, row:end, :] = (k_ref[...] * gk_ref[...]).astype(jnp.bfloat16)
        row = end
    hidden = jnp.concatenate([h_ref[...] for h_ref in h_refs], axis=0)
    value = jnp.dot(hidden, wv_ref[...], preferred_element_type=jnp.float32)
    kv_out[1] = value.astype(jnp.bfloat16)


def finish_projection(groups, w_value, query_gain, key_gain):
    queries, keys, _, hidden = zip(*groups)
    rows, local = sum(q.shape[0] for q in queries), w_value.shape[1]
    return call(
        functools.partial(finish_projection_kernel, len(groups)),
        [*queries, *keys, *hidden, w_value, query_gain, key_gain],
        [like((rows, local)), like((2, rows, local))],
        2 * rows * w_value.size,
    )


def scores_kernel(sizes, ring, offsets, start_ref, q_ref, *refs):
    frames, tokens, sections = sizes
    kv_refs, (scores_ref, values_ref, keys_ref) = refs[:-3], refs[-3:]
    count = len(kv_refs)
    heads, total, columns = scores_ref.shape
    rows = total // len(ring)
    for i, kv_ref in enumerate(kv_refs):
        for j, offset in enumerate(offsets):
            at = pl.multiple_of(i * total + row_of(ring, offset, rows), rows)
            keys_ref[pl.ds(at, rows), :] = kv_ref[0, j * rows : (j + 1) * rows, :]
            values_ref[pl.ds(at, rows), :] = kv_ref[1, j * rows : (j + 1) * rows, :]
    section = lax.axis_index("segment")
    if sections == 2:
        bases = [section, 1 - section]
    else:
        bases = [section, section - 1, section + 1]
    row_frame = lax.broadcasted_iota(jnp.int32, (total, 1), 0) // tokens % frames
    column = lax.broadcasted_iota(jnp.int32, (1, columns), 1)
    column_frame = column // tokens % frames
    key_frame = column_frame + bases[0] * frames
    for i in range(1, count):
        key_frame = jnp.where(column >= i * total, column_frame + bases[i] * frames, key_frame)
    begin = row_frame + section * frames
    for f in range(frames):
        begin = jnp.where(row_frame == f, begin - start_ref[f], begin)
    key_frame = jnp.where((key_frame >= 0) & (key_frame < frames * sections), key_frame, -2 * frames)
    usable = (key_frame >= begin) & (key_frame < begin + KEYWIN)
    for head in range(heads):
        lanes = slice(head * HD, (head + 1) * HD)
        scores = lax.dot_general(
            q_ref[:, lanes], keys_ref[:, lanes], (((1,), (1,)), ((), ())), preferred_element_type=jnp.float32
        )
        scores_ref[head] = jnp.where(usable, scores * HD ** (-0.5), masked_score)


def raw_scores(queries, kv_sets, offsets, ring, window_start, sizes):
    rows, local = queries.shape
    columns = rows * len(kv_sets)
    return call(
        functools.partial(scores_kernel, sizes, ring, tuple(offsets)),
        [window_start, queries, *kv_sets],
        [like((local // HD, rows, columns), jnp.float32), like((columns, local))],
        2 * rows * columns * local,
        scalars=1,
        scratch=[pltpu.VMEM((columns, local), jnp.bfloat16)],
    )


def attend_kernel(ring, inner, offsets, scores_ref, values_ref, sq_ref, out_ref):
    heads, rows, columns = scores_ref.shape
    block = rows // len(offsets)
    inverse_q_row = lax.rsqrt(sq_ref[0:1, :] / inner + epsilon)
    parts = [unplace(inverse_q_row, row_of(ring, offset, block), block) for offset in offsets]
    inverse_q = parts[0] if len(parts) == 1 else jnp.concatenate(parts, axis=0)
    parts = [lax.rsqrt(sq_ref[1 + i : 2 + i, :] / inner + epsilon) for i in range(columns // rows)]
    inverse_k = parts[0] if len(parts) == 1 else jnp.concatenate(parts, axis=1)
    for head in range(heads):
        lanes = slice(head * HD, (head + 1) * HD)
        scores = scores_ref[head] * inverse_q * inverse_k
        lifted = jnp.exp(scores - jnp.max(scores, axis=1, keepdims=True))
        weights = (lifted * (1.0 / jnp.sum(lifted, axis=1, keepdims=True))).astype(jnp.bfloat16)
        out = jnp.dot(weights, values_ref[:, lanes], preferred_element_type=jnp.float32)
        out_ref[:, lanes] = out.astype(jnp.bfloat16)


def attend(scores, values, offsets, ring, squares, inner):
    rows, local = scores.shape[1], values.shape[1]
    return call(
        functools.partial(attend_kernel, ring, inner, tuple(offsets)),
        [scores, values, squares],
        [like((rows, local))],
        2 * rows * values.shape[0] * local,
    )[0]


def partial_kernel(row, att_ref, w_ref, *outs):
    rows = sum(ref.shape[0] for ref in outs)
    out = jnp.dot(att_ref[row : row + rows, :], w_ref[...], preferred_element_type=jnp.float32)
    row = 0
    for ref in outs:
        ref[...] = out[row : row + ref.shape[0]].astype(jnp.bfloat16)
        row += ref.shape[0]


def partials(att, row, w_out, sizes):
    return call(
        functools.partial(partial_kernel, row),
        [att, w_out],
        [like((size, w_out.shape[1])) for size in sizes],
        2 * sum(sizes) * w_out.size,
    )


def next_send_kernel(own_ref, arrived_ref, out_ref):
    total = own_ref[...].astype(jnp.float32) + arrived_ref[...].astype(jnp.float32)
    out_ref[...] = total.astype(jnp.bfloat16)


def next_send(own, arrived):
    return own if arrived is None else call(next_send_kernel, [own, arrived], [like(own.shape)], own.size)[0]


def updated(frame, count, row, x_ref, gate_ref, parts):
    tokens, width = x_ref.shape[1:]
    rows = slice(row, row + count * tokens)
    total = parts[0][rows, :].astype(jnp.float32)
    for part in parts[1:]:
        total = total + part[rows, :].astype(jnp.float32)
    x = x_ref[frame : frame + count].astype(jnp.float32)
    gate = gate_ref[frame : frame + count, :][:, None, :]
    return (x + gate * total.reshape(count, tokens, width)).astype(jnp.bfloat16)


def first_kernel(x_ref, gate_ref, *refs):
    refs[-1][...] = updated(0, 1, 0, x_ref, gate_ref, refs[:-1])[0]


def first_frame(x, gate_rows, parts):
    return call(first_kernel, [x, gate_rows, *parts], [like(x.shape[1:])], 4 * x.size)[0]


def others_kernel(counts, x_ref, gate_ref, *refs):
    parts, out_ref = refs[:-1], refs[-1]
    frames, tokens, _ = x_ref.shape
    half = frames // 2
    out_ref[: half - 1] = updated(1, half - 1, tokens, x_ref, gate_ref, parts[: counts[0]])
    out_ref[half - 1 :] = updated(half, half, 0, x_ref, gate_ref, parts[counts[0] :])


def other_frames(x, gate_rows, near, later):
    frames, tokens, width = x.shape
    counts = (len(near), len(later))
    return call(
        functools.partial(others_kernel, counts),
        [x, gate_rows, *near, *later],
        [like((frames - 1, tokens, width))],
        4 * x.size,
    )[0]


def join_kernel(sections, rest_ref, handed_ref, fresh_ref, out_ref):
    frames = out_ref.shape[0]
    out_ref[: frames - 1] = rest_ref[...]
    newest = lax.axis_index("segment") == sections - 1

    @pl.when(newest)
    def _():
        out_ref[frames - 1 :] = fresh_ref[...]

    @pl.when(jnp.logical_not(newest))
    def _():
        out_ref[frames - 1] = handed_ref[...]


def join(sections, rest, handed, fresh):
    shape = (rest.shape[0] + 1, *rest.shape[1:])
    return call(functools.partial(join_kernel, sections), [rest, handed, fresh], [like(shape)], 1000)[0]


def shards(
    ring,
    queue_frames,
    fresh_frames,
    slot_level,
    window_start,
    shift_table,
    scale_table,
    gate_table,
    w_query,
    w_key,
    w_value,
    w_out,
    query_gain,
    key_gain,
):
    peers = lax.axis_size("seq")
    sections = lax.axis_size("segment")
    frames, tokens, width = queue_frames.shape
    rows = frames * tokens
    half_frames = frames // 2
    local = w_query.shape[1]
    inner = local * peers
    far = peers // 2

    def right(x):
        return lax.ppermute(x, "seq", [(ring[i], ring[(i + 1) % peers]) for i in range(peers)])

    def left(x):
        return lax.ppermute(x, "seq", [(ring[(i + 1) % peers], ring[i]) for i in range(peers)])

    def from_sections(x):
        if sections == 2:
            return [lax.ppermute(x, "segment", [(0, 1), (1, 0)])]
        up = [(i, i + 1) for i in range(sections - 1)]
        return [lax.ppermute(x, "segment", route) for route in (up, [(j, i) for i, j in up])]

    groups, offsets = [], []

    def projected(blocks):
        out = project(*zip(*blocks), ring, scale_rows, shift_rows, weights)
        offsets.append(list(dict.fromkeys(offset for _, offset, _ in blocks)))
        return out

    halves = ((0, half_frames), (half_frames, frames))
    waiting = [(queue_frames, 0, 0)]
    if far > 1:
        arrived = right(queue_frames), left(queue_frames)
    else:
        arrived = right(queue_frames[:half_frames]), left(queue_frames[half_frames:])
    prepared = prepare(
        slot_level,
        [shift_table, scale_table],
        [w_query, w_key],
    )
    arrived, prepared = after(arrived, prepared)
    shift_rows, scale_rows, *weights = prepared
    if far > 1:
        waiting += [(arrived[0], peers - 1, 0), (arrived[1], 1, 0)]
        streams = [[x[lo:hi] for lo, hi in halves] for x in arrived]
    else:
        waiting += [(arrived[0], far, 0), (arrived[1], far, half_frames)]
    for step in range(2, far + 1):
        if step < far:
            moved = [[right(streams[0][i]), left(streams[1][i])] for i in range(2)]
        else:
            moved = [[right(streams[0][0])], [left(streams[1][1])]]
        group = projected(waiting)
        moved[0], group = after(moved[0], group)
        groups.append(group)
        if step < far:
            streams = [[moved[0][i], moved[1][i]] for i in range(2)]
            waiting = [(x, offset, first) for i, offset in ((0, peers - step), (1, step)) for x, (first, _) in zip(streams[i], halves)]
        else:
            waiting = [(moved[0][0], far, 0), (moved[1][0], far, half_frames)]
    groups.append(projected(waiting))
    offsets = sum(offsets, [])

    squares = functools.reduce(jnp.add, [group[2] for group in groups])
    other_squares, groups = after(from_sections(squares[1:2]), groups)
    squares = jnp.concatenate([squares, *other_squares], axis=0)
    queries, kv = finish_projection(groups, w_value, query_gain[None], key_gain[None])
    other_kv = from_sections(kv)
    distance = 1
    while distance < peers:
        pairs = [(i, i ^ distance) for i in range(peers)]
        arrived = lax.ppermute(squares, "seq", pairs)
        if distance == 1:
            arrived, (queries, kv) = after(arrived, (queries, kv))
        elif distance == 2:
            arrived, other_kv = after(arrived, other_kv)
        squares = squares + arrived
        distance *= 2
    scores, all_values = raw_scores(
        queries, [kv, *other_kv], offsets, ring, window_start, (frames, tokens, sections)
    )
    slot_level, _ = after(slot_level, kv)
    (gate_rows,) = prepare(slot_level, [gate_table], [])
    squares, scores, all_values, gate_rows = lax.optimization_barrier((squares, scores, all_values, gate_rows))
    att = attend(scores, all_values, offsets, ring, squares, inner)

    half_rows = rows // 2
    sends = partials(att, offsets.index(far) * rows, w_out, [half_rows] * 2)
    from_left, from_right = [right(sends[0]), None], [None, left(sends[1])]
    out = partials(att, 0, w_out, [half_rows] * (2 * peers - 2))
    own = {offset: out[2 * i : 2 * i + 2] for i, offset in enumerate(offsets[:-1])}
    for step in range(far - 1, 0, -1):
        for to_right, to_left in ((1, 0), (0, 1)):
            from_left[to_right] = right(next_send(own[step][to_right], from_left[to_right]))
            from_right[to_left] = left(next_send(own[peers - step][to_left], from_right[to_left]))
    near, later = (
        [own[0][i]] + [x for x in (from_left[i], from_right[i]) if x is not None] for i in range(2)
    )
    first = first_frame(queue_frames, gate_rows, near)
    handed = lax.ppermute(first, "segment", [(i, i - 1) for i in range(1, sections)])
    rest = other_frames(queue_frames, gate_rows, near, later)
    return (join(sections, rest, handed, fresh_frames), first[None, None])


def ring_order(mesh):
    axes = list(mesh.axis_names)
    index = [0] * len(axes)
    index[axes.index("seq")] = slice(None)
    places = [tuple(d.coords) for d in mesh.devices[tuple(index)]]
    spread = [d for d in range(3) if len({p[d] for p in places}) > 1]
    at = {tuple(p[d] for d in spread): i for i, p in enumerate(places)}
    if len(spread) == 1:
        return [at[key] for key in sorted(at)]
    if len(spread) == 2:
        spans = [sorted({key[i] for key in at}) for i in range(2)]
        long = 0 if len(spans[0]) % 2 == 0 else 1
        if len(spans[long]) % 2 == 0 and len(at) == len(spans[0]) * len(spans[1]):
            outward, across = spans[long], spans[1 - long]
            path = []
            for i, a in enumerate(outward):
                turn = across[1:] if i % 2 == 0 else across[:0:-1]
                path += [(a, b) for b in turn]
            path += [(a, across[0]) for a in reversed(outward)]
            return [at[key if long == 0 else key[::-1]] for key in path]
    return list(range(len(places)))


def solution(mesh):
    return jax.shard_map(
        functools.partial(shards, tuple(ring_order(mesh))),
        mesh=mesh,
        in_specs=(
            P(("groups", "segment"), "seq", None),
            P("groups", "seq", None),
            P(("groups", "segment")),
            P(("groups", "segment")),
            P(),
            P(),
            P(),
            P(None, "seq"),
            P(None, "seq"),
            P(None, "seq"),
            P("seq", None),
            P("seq"),
            P("seq"),
        ),
        out_specs=(
            P(("groups", "segment"), "seq", None),
            P(("groups", "segment"), None, "seq", None),
        ),
        check_vma=False,
    )
```

```python
import functools

import jax
import jax.numpy as jnp
from jax import lax
from jax.experimental import pallas as pl
from jax.experimental.pallas import tpu as pltpu
from jax.sharding import PartitionSpec as P

HD = 128
KEYWIN = 4


epsilon = 1e-06
masked_score = -1e30
VMEM_LIMIT = 16 << 20
WHOLE = pl.BlockSpec(memory_space=pltpu.VMEM)
SCALARS = pl.BlockSpec(memory_space=pltpu.SMEM)


def call(kernel, ins, outs, flops, scalars=0, scratch=(), limit=VMEM_LIMIT):
    moved = sum(x.size * x.dtype.itemsize for x in list(ins) + list(outs))
    return pl.pallas_call(
        kernel,
        in_specs=[SCALARS] * scalars + [WHOLE] * (len(ins) - scalars),
        out_specs=[WHOLE] * len(outs),
        out_shape=list(outs),
        scratch_shapes=list(scratch),
        compiler_params=pltpu.CompilerParams(vmem_limit_bytes=limit),
        cost_estimate=pl.CostEstimate(flops=flops, bytes_accessed=moved, transcendentals=0),
    )(*ins)


def like(shape, dtype=jnp.bfloat16):
    return jax.ShapeDtypeStruct(shape, dtype)


def after(arrived, done):
    return lax.optimization_barrier((arrived, done))


def prepare_kernel(tables, count, level_in, *refs):
    ins, refs = refs[: tables + count], refs[tables + count :]
    rows, kept, scratch = refs[:tables], refs[tables : tables + count], refs[tables + count : 2 * tables + count]
    level_ref, sems = refs[2 * tables + count :]
    pairs = [(level_in, level_ref), *zip(ins, (*scratch, *kept))]
    copies = [pltpu.make_async_copy(src, dst, sems.at[i]) for i, (src, dst) in enumerate(pairs)]
    for copy in copies:
        copy.start()
    for copy in copies[: tables + 1]:
        copy.wait()
    for f in range(rows[0].shape[0]):
        level = level_ref[f]
        for table, out in zip(scratch, rows):
            out[f : f + 1, :] = table[pl.ds(level, 1), :]
    for copy in copies[tables + 1 :]:
        copy.wait()


def prepare(levels, tables, arrays, limit=VMEM_LIMIT):
    in_hbm = pl.BlockSpec(memory_space=pltpu.HBM)
    outs = [like((levels.shape[0], table.shape[1]), table.dtype) for table in tables]
    outs += [like(x.shape, x.dtype) for x in arrays]
    moved = sum(x.size * x.dtype.itemsize for x in (*tables, *arrays))
    return pl.pallas_call(
        functools.partial(prepare_kernel, len(tables), len(arrays)),
        in_specs=[in_hbm] * (1 + len(tables) + len(arrays)),
        out_specs=[WHOLE] * len(outs),
        out_shape=outs,
        scratch_shapes=[pltpu.VMEM(x.shape, x.dtype) for x in tables]
        + [pltpu.SMEM(levels.shape, levels.dtype), pltpu.SemaphoreType.DMA((1 + len(tables) + len(arrays),))],
        compiler_params=pltpu.CompilerParams(vmem_limit_bytes=limit),
        cost_estimate=pl.CostEstimate(flops=1000, bytes_accessed=moved, transcendentals=0),
    )(*(pltpu.with_memory_space_constraint(x, pltpu.HBM) for x in (levels, *tables, *arrays)))


def place(column, first, total):
    rows = column.shape[0]
    lanes = lax.broadcasted_iota(jnp.int32, (rows, total), 1)
    picked = lanes == lax.broadcasted_iota(jnp.int32, (rows, total), 0) + first
    return jnp.sum(jnp.where(picked, column, 0.0), axis=0, keepdims=True)


def unplace(row, first, rows):
    total = row.shape[1]
    lanes = lax.broadcasted_iota(jnp.int32, (rows, total), 1)
    picked = lanes == lax.broadcasted_iota(jnp.int32, (rows, total), 0) + first
    return jnp.sum(jnp.where(picked, row, 0.0), axis=1, keepdims=True)


def row_of(ring, offset, rows):
    index = lax.axis_index("seq")
    first = jnp.int32(0)
    for i, device in enumerate(ring):
        first = jnp.where(index == device, (i + offset) % len(ring) * rows, first)
    return pl.multiple_of(first, rows)


def project_kernel(first_frames, offsets, ring, *refs):
    count = len(first_frames)
    x_refs, refs = refs[:count], refs[count:]
    scale_ref, shift_ref, wq_ref, wk_ref, q_ref, k_ref, sq_ref, h_ref = refs
    row = 0
    for x_ref, first in zip(x_refs, first_frames):
        frames, tokens, width = x_ref.shape
        x = x_ref[...].astype(jnp.float32)
        inverse = lax.rsqrt(jnp.mean(x * x, axis=2, keepdims=True) + epsilon)
        scale = 1.0 + scale_ref[first : first + frames, :][:, None, :]
        shift = shift_ref[first : first + frames, :][:, None, :]
        hidden = (x * inverse * scale + shift).astype(jnp.bfloat16)
        h_ref[row : row + frames * tokens, :] = hidden.reshape(frames * tokens, width)
        row += frames * tokens
    rows = row // len(offsets)
    total = sq_ref.shape[1]
    hidden = h_ref[...]

    def squares_of(raw):
        column = jnp.sum(raw * raw, axis=1, keepdims=True)
        parts = [
            place(column[i * rows : (i + 1) * rows], row_of(ring, offset, rows), total)
            for i, offset in enumerate(offsets)
        ]
        return sum(parts[1:], parts[0])

    q_raw = jnp.dot(hidden, wq_ref[...], preferred_element_type=jnp.float32)
    sq_ref[0:1, :] = squares_of(q_raw)
    q_ref[...] = q_raw
    k_raw = jnp.dot(hidden, wk_ref[...], preferred_element_type=jnp.float32)
    sq_ref[1:2, :] = squares_of(k_raw)
    k_ref[...] = k_raw


def project(blocks, offsets, first_frames, ring, scale_rows, shift_rows, weights):
    w_query, w_key = weights
    width, local = w_query.shape
    offsets = dict.fromkeys(offsets)
    rows = sum(x.shape[0] * x.shape[1] for x in blocks)
    total = rows // len(offsets) * len(ring)
    return call(
        functools.partial(project_kernel, tuple(first_frames), tuple(offsets), ring),
        [*blocks, scale_rows, shift_rows, w_query, w_key],
        [like((rows, local), jnp.float32)] * 2 + [like((2, total), jnp.float32), like((rows, width))],
        4 * rows * width * local,
    )


def finish_projection_kernel(count, *refs):
    q_refs, k_refs, h_refs = (refs[i * count : (i + 1) * count] for i in range(3))
    wv_ref, gq_ref, gk_ref, q_out, kv_out = refs[3 * count :]
    row = 0
    for q_ref, k_ref in zip(q_refs, k_refs):
        end = row + q_ref.shape[0]
        q_out[row:end, :] = (q_ref[...] * gq_ref[...]).astype(jnp.bfloat16)
        kv_out[0, row:end, :] = (k_ref[...] * gk_ref[...]).astype(jnp.bfloat16)
        row = end
    hidden = jnp.concatenate([h_ref[...] for h_ref in h_refs], axis=0)
    value = jnp.dot(hidden, wv_ref[...], preferred_element_type=jnp.float32)
    kv_out[1] = value.astype(jnp.bfloat16)


def finish_projection(groups, w_value, query_gain, key_gain):
    queries, keys, _, hidden = zip(*groups)
    rows, local = sum(q.shape[0] for q in queries), w_value.shape[1]
    return call(
        functools.partial(finish_projection_kernel, len(groups)),
        [*queries, *keys, *hidden, w_value, query_gain, key_gain],
        [like((rows, local)), like((2, rows, local))],
        2 * rows * w_value.size,
    )


def scores_kernel(sizes, ring, offsets, start_ref, q_ref, *refs):
    frames, tokens, sections = sizes
    kv_refs, (scores_ref, values_ref, keys_ref) = refs[:-3], refs[-3:]
    count = len(kv_refs)
    heads, total, columns = scores_ref.shape
    rows = total // len(ring)
    for i, kv_ref in enumerate(kv_refs):
        for j, offset in enumerate(offsets):
            at = pl.multiple_of(i * total + row_of(ring, offset, rows), rows)
            keys_ref[pl.ds(at, rows), :] = kv_ref[0, j * rows : (j + 1) * rows, :]
            values_ref[pl.ds(at, rows), :] = kv_ref[1, j * rows : (j + 1) * rows, :]
    section = lax.axis_index("segment")
    if sections == 2:
        bases = [section, 1 - section]
    else:
        bases = [section, section - 1, section + 1]
    row_frame = lax.broadcasted_iota(jnp.int32, (total, 1), 0) // tokens % frames
    column = lax.broadcasted_iota(jnp.int32, (1, columns), 1)
    column_frame = column // tokens % frames
    key_frame = column_frame + bases[0] * frames
    for i in range(1, count):
        key_frame = jnp.where(column >= i * total, column_frame + bases[i] * frames, key_frame)
    begin = row_frame + section * frames
    for f in range(frames):
        begin = jnp.where(row_frame == f, begin - start_ref[f], begin)
    key_frame = jnp.where((key_frame >= 0) & (key_frame < frames * sections), key_frame, -2 * frames)
    usable = (key_frame >= begin) & (key_frame < begin + KEYWIN)
    for head in range(heads):
        lanes = slice(head * HD, (head + 1) * HD)
        scores = lax.dot_general(
            q_ref[:, lanes], keys_ref[:, lanes], (((1,), (1,)), ((), ())), preferred_element_type=jnp.float32
        )
        scores_ref[head] = jnp.where(usable, scores * HD ** (-0.5), masked_score)


def raw_scores(queries, kv_sets, offsets, ring, window_start, sizes):
    rows, local = queries.shape
    columns = rows * len(kv_sets)
    return call(
        functools.partial(scores_kernel, sizes, ring, tuple(offsets)),
        [window_start, queries, *kv_sets],
        [like((local // HD, rows, columns), jnp.float32), like((columns, local))],
        2 * rows * columns * local,
        scalars=1,
        scratch=[pltpu.VMEM((columns, local), jnp.bfloat16)],
    )


def attend_kernel(ring, inner, first, offsets, scores_ref, values_ref, sq_ref, out_ref):
    heads, total, columns = scores_ref.shape
    rows = out_ref.shape[0]
    block = rows // len(offsets)
    inverse_q_row = lax.rsqrt(sq_ref[0:1, :] / inner + epsilon)
    parts = [unplace(inverse_q_row, row_of(ring, offset, block), block) for offset in offsets]
    inverse_q = parts[0] if len(parts) == 1 else jnp.concatenate(parts, axis=0)
    parts = [lax.rsqrt(sq_ref[1 + i : 2 + i, :] / inner + epsilon) for i in range(columns // total)]
    inverse_k = parts[0] if len(parts) == 1 else jnp.concatenate(parts, axis=1)
    for head in range(heads):
        lanes = slice(head * HD, (head + 1) * HD)
        scores = scores_ref[head, first : first + rows, :] * inverse_q * inverse_k
        lifted = jnp.exp(scores - jnp.max(scores, axis=1, keepdims=True))
        weights = (lifted * (1.0 / jnp.sum(lifted, axis=1, keepdims=True))).astype(jnp.bfloat16)
        out = jnp.dot(weights, values_ref[:, lanes], preferred_element_type=jnp.float32)
        out_ref[:, lanes] = out.astype(jnp.bfloat16)


def attend(scores, values, first, offsets, ring, squares, inner):
    rows, local = scores.shape[1] // len(ring) * len(offsets), values.shape[1]
    return call(
        functools.partial(attend_kernel, ring, inner, first, tuple(offsets)),
        [scores, values, squares],
        [like((rows, local))],
        2 * rows * values.shape[0] * local,
    )[0]


def partial_kernel(att_ref, w_ref, *outs):
    out = jnp.dot(att_ref[...], w_ref[...], preferred_element_type=jnp.float32)
    row = 0
    for ref in outs:
        ref[...] = out[row : row + ref.shape[0]].astype(jnp.bfloat16)
        row += ref.shape[0]


def partials(att, w_out, sizes):
    return call(
        partial_kernel,
        [att, w_out],
        [like((size, w_out.shape[1])) for size in sizes],
        2 * sum(sizes) * w_out.size,
    )


def next_send_kernel(own_ref, arrived_ref, out_ref):
    total = own_ref[...].astype(jnp.float32) + arrived_ref[...].astype(jnp.float32)
    out_ref[...] = total.astype(jnp.bfloat16)


def next_send(own, arrived):
    return own if arrived is None else call(next_send_kernel, [own, arrived], [like(own.shape)], own.size)[0]


def updated(frame, count, row, x_ref, gate_ref, parts):
    tokens, width = x_ref.shape[1:]
    rows = slice(row, row + count * tokens)
    total = parts[0][rows, :].astype(jnp.float32)
    for part in parts[1:]:
        total = total + part[rows, :].astype(jnp.float32)
    x = x_ref[frame : frame + count].astype(jnp.float32)
    gate = gate_ref[frame : frame + count, :][:, None, :]
    return (x + gate * total.reshape(count, tokens, width)).astype(jnp.bfloat16)


def first_kernel(x_ref, gate_ref, *refs):
    refs[-1][...] = updated(0, 1, 0, x_ref, gate_ref, refs[:-1])[0]


def first_frame(x, gate_rows, parts):
    return call(first_kernel, [x, gate_rows, *parts], [like(x.shape[1:])], 4 * x.size)[0]


def others_kernel(counts, sections, x_ref, gate_ref, handed_ref, fresh_ref, *refs):
    parts, out_ref = refs[:-1], refs[-1]
    frames, tokens, _ = x_ref.shape
    half = frames // 2
    out_ref[: half - 1] = updated(1, half - 1, tokens, x_ref, gate_ref, parts[: counts[0]])
    out_ref[half - 1 : frames - 1] = updated(half, half, 0, x_ref, gate_ref, parts[counts[0] :])
    newest = lax.axis_index("segment") == sections - 1

    @pl.when(newest)
    def _():
        out_ref[frames - 1 :] = fresh_ref[...]

    @pl.when(jnp.logical_not(newest))
    def _():
        out_ref[frames - 1] = handed_ref[...]


def next_queue(x, gate_rows, handed, fresh, near, later, sections):
    return call(
        functools.partial(others_kernel, (len(near), len(later)), sections),
        [x, gate_rows, handed, fresh, *near, *later],
        [like(x.shape)],
        4 * x.size,
    )[0]


def shards(
    ring,
    queue_frames,
    fresh_frames,
    slot_level,
    window_start,
    shift_table,
    scale_table,
    gate_table,
    w_query,
    w_key,
    w_value,
    w_out,
    query_gain,
    key_gain,
):
    peers = lax.axis_size("seq")
    sections = lax.axis_size("segment")
    frames, tokens, width = queue_frames.shape
    rows = frames * tokens
    half_frames = frames // 2
    local = w_query.shape[1]
    inner = local * peers
    far = peers // 2

    def right(x):
        return lax.ppermute(x, "seq", [(ring[i], ring[(i + 1) % peers]) for i in range(peers)])

    def left(x):
        return lax.ppermute(x, "seq", [(ring[(i + 1) % peers], ring[i]) for i in range(peers)])

    def from_sections(x, pairs=None):
        if sections == 2:
            routes = [[(0, 1), (1, 0)]]
        else:
            up = [(i, i + 1) for i in range(sections - 1)]
            routes = [up, [(j, i) for i, j in up]]
        if pairs is None:
            return [lax.ppermute(x, "segment", route) for route in routes]
        joint = [[(i * sections + k, j * sections + l) for i, j in pairs for k, l in route] for route in routes]
        return [lax.ppermute(x, ("seq", "segment"), route) for route in joint]

    groups, offsets = [], []

    def projected(blocks):
        out = project(*zip(*blocks), ring, scale_rows, shift_rows, weights)
        offsets.append(list(dict.fromkeys(offset for _, offset, _ in blocks)))
        return out

    halves = (queue_frames[:half_frames], queue_frames[half_frames:])
    firsts = (0, half_frames)
    waiting = [(queue_frames, 0, 0)]
    to_right, to_left = list(halves), list(halves)
    for step in range(1, far + 1):
        lead = right(to_right[0]), left(to_left[1])
        if step < far:
            lag = right(to_right[1]), left(to_left[0])
        if step == 1:
            prepared = prepare(slot_level, [shift_table, scale_table], [w_query, w_key])
            lead, prepared = after(lead, prepared)
            shift_rows, scale_rows, *weights = prepared
        else:
            group = projected(waiting)
            lead, group = after(lead, group)
            groups.append(group)
            waiting = []
        if step < far:
            to_right, to_left = [lead[0], lag[0]], [lag[1], lead[1]]
            for blocks, offset in ((to_right, peers - step), (to_left, step)):
                waiting += [(x, offset, first) for x, first in zip(blocks, firsts)]
        else:
            waiting += [(x, far, first) for x, first in zip(lead, firsts)]
    groups.append(projected(waiting))
    offsets = sum(offsets, [])

    own = functools.reduce(jnp.add, [group[2] for group in groups])
    distance = 1
    while distance < peers:
        pairs = [(i, i ^ distance) for i in range(peers)]
        if distance == 1:
            arrived = lax.ppermute(own, "seq", pairs)
            near = from_sections(own[1:2])
            away = from_sections(own[1:2], pairs)
            arrived, near, away, groups = lax.optimization_barrier((arrived, near, away, groups))
            own = jnp.concatenate([own + arrived] + [x + y for x, y in zip(near, away)], axis=0)
        else:
            arrived = lax.ppermute(own, "seq", pairs)
            if distance == 2:
                queries, kv = finish_projection(groups, w_value, query_gain[None], key_gain[None])
                arrived, (queries, kv) = after(arrived, (queries, kv))
                other_kv = from_sections(kv)
            own = own + arrived
        distance *= 2
    squares = own
    scores, all_values = raw_scores(
        queries, [kv, *other_kv], offsets, ring, window_start, (frames, tokens, sections)
    )
    slot_level, _ = after(slot_level, kv)
    (gate_rows,) = prepare(slot_level, [gate_table], [])
    squares, scores, all_values, gate_rows = lax.optimization_barrier((squares, scores, all_values, gate_rows))

    def attended(first, last):
        return attend(scores, all_values, first * rows, offsets[first:last], ring, squares, inner)

    half_rows = rows // 2
    sends = partials(attended(peers - 1, peers), w_out, [half_rows] * 2)
    from_left, from_right = [right(sends[0]), None], [None, left(sends[1])]
    out = partials(attended(0, peers - 1), w_out, [half_rows] * (2 * peers - 2))
    own = {offset: out[2 * i : 2 * i + 2] for i, offset in enumerate(offsets[:-1])}
    for step in range(far - 1, 0, -1):
        for to_right, to_left in ((1, 0), (0, 1)):
            from_left[to_right] = right(next_send(own[step][to_right], from_left[to_right]))
            from_right[to_left] = left(next_send(own[peers - step][to_left], from_right[to_left]))
    near, later = (
        [own[0][i]] + [x for x in (from_left[i], from_right[i]) if x is not None] for i in range(2)
    )
    first = first_frame(queue_frames, gate_rows, near)
    handed = lax.ppermute(first, "segment", [(i, i - 1) for i in range(1, sections)])
    return (
        next_queue(queue_frames, gate_rows, handed, fresh_frames, near, later, sections),
        first[None, None],
    )


def ring_order(mesh):
    axes = list(mesh.axis_names)
    index = [0] * len(axes)
    index[axes.index("seq")] = slice(None)
    places = [tuple(d.coords) for d in mesh.devices[tuple(index)]]
    spread = [d for d in range(3) if len({p[d] for p in places}) > 1]
    at = {tuple(p[d] for d in spread): i for i, p in enumerate(places)}
    if len(spread) == 1:
        return [at[key] for key in sorted(at)]
    if len(spread) == 2:
        spans = [sorted({key[i] for key in at}) for i in range(2)]
        long = 0 if len(spans[0]) % 2 == 0 else 1
        if len(spans[long]) % 2 == 0 and len(at) == len(spans[0]) * len(spans[1]):
            outward, across = spans[long], spans[1 - long]
            path = []
            for i, a in enumerate(outward):
                turn = across[1:] if i % 2 == 0 else across[:0:-1]
                path += [(a, b) for b in turn]
            path += [(a, across[0]) for a in reversed(outward)]
            return [at[key if long == 0 else key[::-1]] for key in path]
    return list(range(len(places)))


def solution(mesh):
    return jax.shard_map(
        functools.partial(shards, tuple(ring_order(mesh))),
        mesh=mesh,
        in_specs=(
            P(("groups", "segment"), "seq", None),
            P("groups", "seq", None),
            P(("groups", "segment")),
            P(("groups", "segment")),
            P(),
            P(),
            P(),
            P(None, "seq"),
            P(None, "seq"),
            P(None, "seq"),
            P("seq", None),
            P("seq"),
            P("seq"),
        ),
        out_specs=(
            P(("groups", "segment"), "seq", None),
            P(("groups", "segment"), None, "seq", None),
        ),
        check_vma=False,
    )
```
